32 devices in a mesh: ctx: 4 (over z), ep: 8 (over y, x, core).
Axes of the slice: x: 2, y: 2, z: 4, core: 2. Of those that a mesh axis runs over, the one named last changes fastest.
Arguments:
- out_grad: bfloat16 [64, 3584], P(('ctx', 'ep')), may hold values from -6 to 6
- expert_ids: int32 [64, 8], P(('ctx', 'ep')), may hold values from 0 to 31, all different within a row; in each aligned block of 16 rows (0 to 15, 16 to 31, ...) at most 7 rows name the same one
- gate_values: float32 [64, 8], P(('ctx', 'ep')), may hold values from 0.1 to 2.5
- hidden: bfloat16 [4, 32, 7, 1536], P(None, 'ep', None, 'ctx'), may hold values from -0.29882812 to 0.29882812
- w_down: bfloat16 [32, 1536, 3584], P('ep', 'ctx'), may hold values from -0.15625 to 0.15625
Outputs:
- hidden_grad: bfloat16 [4, 32, 7, 1536], P(None, 'ep', None, 'ctx')
- weight_grad: bfloat16 [32, 1536, 3584], P('ep', 'ctx')
- gate_grad: float32 [64, 8], P(('ctx', 'ep'))
The draws below stay inside these ranges and needn't reach their ends.
Inputs may be any that keep to these rules, and one draw needn't show every extreme that they name: `expert_ids`: each token names 8 different experts. In each aligned block of 16 tokens no expert is named by more than 7 tokens.
All inputs are finite; a program needn't handle non-finite values.
Results may differ from the reference program's by a relative error of at most 0.012.
Values may be sent and summed in bfloat16 or wider, within the bound.
A program may use at most 64 MiB of HBM per device.

```python
import math
import jax
import jax.numpy as jnp
import numpy as np
from jax import lax

D = 3584
F = 1536
TOPK = 8
EXPERTS = 32
CAPACITY = 7
GROUPS = 4
GROUP_TOK = 16
TOKENS = 64


def level_of(stream_key, extent, pieces, low, high):
    factor_of, own = 1.0, jax.random.fold_in(stream_key, 6)
    for axis_at, parts in pieces:
        heights = jnp.exp(jax.random.uniform(jax.random.fold_in(own, axis_at), (parts,), jnp.float32, low / len(pieces), high / len(pieces)))
        factor_of = factor_of * jnp.repeat(heights, extent[axis_at] // parts).reshape([-1 if axis == axis_at else 1 for axis in range(len(extent))])
    return factor_of


def routed_block(key, own, number, rows, amount, top, most, lean):
    order = jax.random.permutation(key, amount)
    heavy_load, common = portions_of(amount, rows * top, most, lean, True), portions_of(amount, rows * top, most, lean, False)
    places = jnp.arange(amount)

    def named(tallies, offset_by):
        used = int((tallies > 0).sum())
        fixed = max(1, used // 4)
        moved = fixed + (places - fixed + offset_by * (used - fixed)) % max(1, amount - fixed)
        return jnp.zeros((amount,), jnp.int32).at[order[jnp.where(places < fixed, places, moved)]].set(jnp.asarray(tallies, jnp.int32))

    tallies = jnp.where(number % 4 == 0, named(heavy_load, number // 4), named(common, number - number // 4 - 1))
    mixed = jax.random.permutation(jax.random.fold_in(own, 3), amount)
    donor, sink = mixed[0:amount // 2 * 2:2], mixed[1:amount // 2 * 2:2]
    room = jnp.minimum(tallies[donor] - 1, most - tallies[sink]) // 2
    room = jnp.where((donor == order[0]) | (sink == order[0]) | (tallies[sink] == 0), 0, jnp.maximum(room, 0))
    moved = jax.random.randint(jax.random.fold_in(own, 4), (amount // 2,), 0, 1 << 20) % (room + 1)
    tallies = tallies.at[donor].add(-moved).at[sink].add(moved)
    labels = jnp.searchsorted(jnp.cumsum(tallies), jnp.arange(rows * top), side="right").astype(jnp.int32)
    table = labels.reshape(top, rows).T
    table = table[jax.random.permutation(jax.random.fold_in(own, 1), rows)]
    offset_by = jax.random.randint(jax.random.fold_in(own, 2), (rows, 1), 0, top)
    return jnp.take_along_axis(table, (jnp.arange(top)[None, :] + offset_by) % top, axis=1)


def portions_of(number_of, total, most, slope, full):
    portions = [(1 << 20) // math.isqrt(standing ** slope) + 1 for standing in range(1, number_of + 1)]
    largest = most if full else min(most, max(-(-total // number_of), total * portions[0] // sum(portions)))
    least = 1 if total - largest >= number_of - 1 else 0
    counts, surplus = [largest] + [least] * (number_of - 1), total - largest - least * (number_of - 1)
    while surplus > 0:
        movable = [i for i in range(1, number_of) if counts[i] < largest] or [i for i in range(1, number_of) if counts[i] < most]
        mass, remaining = sum([portions[i] for i in movable]), surplus
        for i in movable:
            extra = min(most - counts[i], max(1, remaining * portions[i] // mass), surplus)
            counts[i] = counts[i] + extra
            surplus = surplus - extra
    return np.array(counts)


def scatter_about(stream_key, dims, spread, bound, shards=(), kind=jnp.bfloat16):
    values = spread * jax.random.normal(stream_key, dims, jnp.float32)
    if shards:
        values = values * level_of(stream_key, dims, shards, -0.22, 0.18)
    return jnp.clip(values, -bound, bound).astype(kind)


def setup_inputs(seed: int = 0) -> dict:
    splits = jax.random.split(jax.random.key(seed), 6)
    out_grad = scatter_about(splits[0], (TOKENS, D), 1.0, 6.0, ((0, 32),))
    expert_ids_keys = jax.random.split(jax.random.fold_in(splits[1], 1), TOKENS // GROUP_TOK)
    expert_ids_turns = jax.random.permutation(jax.random.fold_in(splits[1], 3), TOKENS // GROUP_TOK)
    expert_ids = jax.vmap(lambda own, number: routed_block(jax.random.fold_in(splits[1], 2), own, number, GROUP_TOK, EXPERTS, TOPK, CAPACITY, 2))(expert_ids_keys, expert_ids_turns).reshape((TOKENS, TOPK))
    gate_values = jnp.clip(jnp.exp(math.log(2.5) - 3.218876 * jax.random.uniform(splits[2], (TOKENS, TOPK), jnp.float32) ** level_of(splits[2], (TOKENS, TOPK), ((0, 32),), -0.2, 0.2)), 0.1, 2.5)
    hidden = scatter_about(splits[3], (GROUPS, EXPERTS, CAPACITY, F), 0.05, 0.29882812, ((1, 8), (3, 4)))
    w_down = scatter_about(splits[4], (EXPERTS, F, D), F ** -0.5, 0.15625, ((0, 8), (1, 4)))
    return {"out_grad": out_grad, "expert_ids": expert_ids, "gate_values": gate_values, "hidden": hidden, "w_down": w_down}


def route_slots(expert_ids):
    group_routes = GROUP_TOK * TOPK
    group_ids = expert_ids.reshape(GROUPS, group_routes)
    onehot = (group_ids[:, :, None] == jnp.arange(EXPERTS, dtype=jnp.int32)[None, None, :]).astype(jnp.int32)
    before = jnp.cumsum(onehot, axis=1) - onehot
    slot_index = jnp.sum(before * onehot, axis=2).astype(jnp.int32)
    return group_ids, slot_index


def reference(out_grad, expert_ids, gate_values, hidden, w_down):
    group_routes = GROUP_TOK * TOPK
    group_ids, slot_index = route_slots(expert_ids)
    place = (group_ids * CAPACITY + slot_index).astype(jnp.int32)
    group_base = (jnp.arange(GROUPS, dtype=jnp.int32) * GROUP_TOK)[:, None]
    token_index = group_base + (jnp.arange(group_routes, dtype=jnp.int32) // TOPK)[None, :]
    group_index = jnp.broadcast_to(jnp.arange(GROUPS, dtype=jnp.int32)[:, None], place.shape)
    slot_token = jnp.zeros((GROUPS, EXPERTS * CAPACITY), jnp.int32).at[group_index, place].set(token_index + 1)
    slot_gate = jnp.zeros((GROUPS, EXPERTS * CAPACITY), jnp.float32).at[group_index, place].set(
        gate_values.reshape(GROUPS, group_routes))
    slot_token = slot_token.reshape(GROUPS, EXPERTS, CAPACITY)
    slot_gate = slot_gate.reshape(GROUPS, EXPERTS, CAPACITY)

    def one_expert(expert):
        token_pick = slot_token[:, expert, :].reshape(-1)
        gate_pick = slot_gate[:, expert, :].reshape(-1)
        live_mask = token_pick > 0
        safe_index = jnp.maximum(token_pick - 1, 0).astype(jnp.int32)
        slot_rows = jnp.where(live_mask[:, None], out_grad[safe_index], jnp.zeros((), out_grad.dtype))
        weight = w_down[expert]
        grad_in = jnp.dot(slot_rows, weight.T, preferred_element_type=jnp.float32)
        saved_hid = hidden[:, expert].reshape(GROUPS * CAPACITY, F)
        hid_grad = (gate_pick[:, None] * grad_in).astype(jnp.bfloat16)
        gate_slot = jnp.sum(saved_hid.astype(jnp.float32) * grad_in, axis=1)
        scaled = (gate_pick[:, None] * slot_rows.astype(jnp.float32)).astype(jnp.bfloat16)
        weight_sum = jnp.dot(saved_hid.T, scaled, preferred_element_type=jnp.float32)
        return hid_grad.reshape(GROUPS, CAPACITY, F), gate_slot.reshape(GROUPS, CAPACITY), weight_sum.astype(jnp.bfloat16)

    hid_all, gate_all, weight_grad = lax.map(one_expert, jnp.arange(EXPERTS, dtype=jnp.int32))
    hidden_grad = jnp.transpose(hid_all, (1, 0, 2, 3))
    gate_table = jnp.transpose(gate_all, (1, 0, 2)).reshape(GROUPS, EXPERTS * CAPACITY)
    gate_grad = jnp.take_along_axis(gate_table, place, axis=1).reshape(TOKENS, TOPK)
    return hidden_grad, weight_grad, gate_grad
```

```python
import functools
import jax
import jax.numpy as jnp
from jax import lax
from jax.experimental import pallas as pl
from jax.experimental.pallas import tpu as pltpu
from jax.sharding import PartitionSpec as P

LANES = 128
VMEM_BUDGET = 40 << 20
MESH = pl.DeviceIdType.MESH
HIGHEST = lax.Precision.HIGHEST


def exchange_kernel(
    sizes, pack_ref, hid_ref, w_ref,
    hid_grad_ref, by_token_ref, rows_ref, gates_ref, route_ref,
    rows_in, w_in, part, parts_in,
    w_sem, own_sem, send_sem, recv_sem, send2_sem, recv2_sem,
):
    ctx_count, ep_count, tok_dev, top, groups, exp_dev, capacity, width = sizes
    count = ctx_count * ep_count
    tokens = count * tok_dev
    group_tok = tokens // groups
    features = rows_ref.shape[1]
    ctx, ep = lax.axis_index("ctx"), lax.axis_index("ep")
    me = ctx * ep_count + ep
    weights = [
        pltpu.make_async_copy(w_ref.at[e], w_in.at[e], w_sem.at[e]) for e in range(exp_dev)
    ]
    for copy in weights:
        copy.start()
    own = pltpu.make_async_copy(pack_ref, rows_in.at[me], own_sem)
    own.start()

    peers = []
    for step in range(1, count):
        peer = lax.rem(me + step, count)
        peers.append((peer // ep_count, lax.rem(peer, ep_count)))
    barrier = pltpu.get_barrier_semaphore()
    for peer in peers:
        pl.semaphore_signal(barrier, inc=1, device_id=peer, device_id_type=MESH)
    pl.semaphore_wait(barrier, count - 1)
    sends = [
        pltpu.make_async_remote_copy(
            src_ref=pack_ref, dst_ref=rows_in.at[me], send_sem=send_sem.at[i],
            recv_sem=recv_sem.at[i], device_id=peer, device_id_type=MESH,
        )
        for i, peer in enumerate(peers)
    ]
    for copy in sends:
        copy.start()

    pad = 8
    hid = []
    for e in range(exp_dev):
        pieces = []
        for g in range(groups):
            piece = hid_ref[g, e].astype(jnp.float32)
            pieces.append(
                jnp.concatenate([piece, jnp.zeros((pad - capacity, width), jnp.float32)], axis=0)
            )
        hid.append(jnp.concatenate(pieces, axis=0))

    own.wait()
    for copy in sends:
        copy.wait_recv()

    gathered = rows_in[...].reshape(tokens, features + LANES)
    rows_ref[...] = gathered[:, :features]
    meta = gathered[:, features:].astype(jnp.float32)
    meta_t = meta.T
    ids_t = meta_t[:top].astype(jnp.int32)
    gates_t = meta_t[top:2 * top]
    tok_a = lax.broadcasted_iota(jnp.int32, (tokens, tokens), 0)
    tok_b = lax.broadcasted_iota(jnp.int32, (tokens, tokens), 1)
    earlier = ((tok_a < tok_b) & (tok_a // group_tok == tok_b // group_tok)).astype(jnp.float32)
    row_slot = lax.broadcasted_iota(jnp.int32, (groups * pad, tokens), 0)
    row_group = lax.broadcasted_iota(jnp.int32, (groups * pad, tokens), 1) // group_tok

    members, gate_rows = [], []
    for e in range(exp_dev):
        named = ids_t == ep * exp_dev + e
        members.append(jnp.sum(jnp.where(named, 1.0, 0.0), axis=0, keepdims=True))
        gate_rows.append(jnp.sum(jnp.where(named, gates_t, 0.0), axis=0, keepdims=True))
    member = jnp.concatenate(members + [jnp.zeros((8 - exp_dev, tokens), jnp.float32)], axis=0)
    gate = jnp.concatenate(gate_rows + [jnp.zeros((8 - exp_dev, tokens), jnp.float32)], axis=0)
    slots = jnp.dot(member, earlier, preferred_element_type=jnp.float32).astype(jnp.int32)
    gates_ref[...] = jnp.concatenate(
        [gate, jnp.zeros((LANES - 8, tokens), jnp.float32)], axis=0
    ).T

    rows = rows_ref[...]
    for e in range(exp_dev):
        place = jnp.where(member[e:e + 1] > 0, row_group[:1] * pad + slots[e:e + 1], -1)
        pick = jnp.where(row_slot == place, 1.0, 0.0)
        by_token = lax.dot_general(
            hid[e].astype(jnp.bfloat16), pick.astype(jnp.bfloat16), (((0,), (0,)), ((), ())),
            preferred_element_type=jnp.float32,
        )
        by_token_ref[e] = by_token.astype(jnp.bfloat16)
        weights[e].wait()
        grad = lax.dot_general(
            w_in[e], rows, (((1,), (1,)), ((), ())), preferred_element_type=jnp.float32
        )
        part[e:e + 1, :] = jnp.sum(by_token * grad, axis=0, keepdims=True)
        gated = grad * gate[e:e + 1]
        slot_grad = lax.dot_general(
            pick.astype(jnp.bfloat16), gated.astype(jnp.bfloat16), (((1,), (1,)), ((), ())),
            preferred_element_type=jnp.float32,
        )
        for g in range(groups):
            hid_grad_ref[g, e] = slot_grad[g * pad:g * pad + capacity].astype(jnp.bfloat16)

    returns = [
        pltpu.make_async_remote_copy(
            src_ref=part, dst_ref=parts_in.at[me], send_sem=send2_sem.at[i],
            recv_sem=recv2_sem.at[i], device_id=peer, device_id_type=MESH,
        )
        for i, peer in enumerate(peers)
    ]
    for copy in returns:
        copy.start()
    for copy in sends:
        copy.wait_send()
    for copy in returns:
        copy.wait_recv()
    mine = part[...]
    result = jnp.zeros((top, tokens), jnp.float32)
    for p in range(ep_count):
        total = jnp.zeros(mine.shape, jnp.float32)
        for c in range(ctx_count):
            d = c * ep_count + p
            total = total + jnp.where(d == me, mine, parts_in[d])
        for e in range(exp_dev):
            result = result + jnp.where(ids_t == p * exp_dev + e, total[e:e + 1], 0.0)
    route_ref[...] = result
    for copy in returns:
        copy.wait_send()


def weight_kernel(exp_dev, chunk, by_token_ref, rows_ref, gates_ref, out_ref):
    lane = lax.broadcasted_iota(jnp.int32, gates_ref.shape, 1)
    gate = jnp.sum(
        jnp.where(lane == pl.program_id(0), gates_ref[...], 0.0), axis=1, keepdims=True
    )
    left = by_token_ref[0]
    for at in range(0, out_ref.shape[2], chunk):
        scaled = (gate * rows_ref[:, at:at + chunk].astype(jnp.float32)).astype(jnp.bfloat16)
        out_ref[0, :, at:at + chunk] = jnp.dot(
            left, scaled, preferred_element_type=jnp.float32
        ).astype(jnp.bfloat16)


def fused_device(out_grad, expert_ids, gate_values, hidden, w_down):
    tok_dev, top = expert_ids.shape
    groups, exp_dev, capacity, width = hidden.shape
    features = out_grad.shape[1]
    ctx_count, ep_count = lax.axis_size("ctx"), lax.axis_size("ep")
    count = ctx_count * ep_count
    tokens = count * tok_dev
    pack = jnp.concatenate(
        [
            out_grad,
            expert_ids.astype(jnp.bfloat16),
            gate_values.astype(jnp.bfloat16),
            jnp.zeros((tok_dev, LANES - 2 * top), jnp.bfloat16),
        ],
        axis=1,
    )
    sizes = (ctx_count, ep_count, tok_dev, top, groups, exp_dev, capacity, width)
    vmem = pl.BlockSpec(memory_space=pltpu.VMEM)
    hid_grad, by_token, rows, gates, routes = pl.pallas_call(
        functools.partial(exchange_kernel, sizes),
        out_shape=(
            jax.ShapeDtypeStruct(hidden.shape, jnp.bfloat16),
            jax.ShapeDtypeStruct((exp_dev, width, tokens), jnp.bfloat16),
            jax.ShapeDtypeStruct((tokens, features), jnp.bfloat16),
            jax.ShapeDtypeStruct((tokens, LANES), jnp.float32),
            jax.ShapeDtypeStruct((top, tokens), jnp.float32),
        ),
        in_specs=[vmem, vmem, pl.BlockSpec(memory_space=pl.ANY)],
        out_specs=(vmem,) * 5,
        scratch_shapes=[
            pltpu.VMEM((count, tok_dev, features + LANES), jnp.bfloat16),
            pltpu.VMEM(w_down.shape, jnp.bfloat16),
            pltpu.VMEM((exp_dev, tokens), jnp.float32),
            pltpu.VMEM((count, exp_dev, tokens), jnp.float32),
            pltpu.SemaphoreType.DMA((exp_dev,)),
            pltpu.SemaphoreType.DMA,
            pltpu.SemaphoreType.DMA((count - 1,)),
            pltpu.SemaphoreType.DMA((count - 1,)),
            pltpu.SemaphoreType.DMA((count - 1,)),
            pltpu.SemaphoreType.DMA((count - 1,)),
        ],
        compiler_params=pltpu.CompilerParams(
            collective_id=0, has_side_effects=True, vmem_limit_bytes=56 << 20
        ),
        name="exchange",
    )(pack, hidden, w_down)
    chunk = features
    for pieces in range(1, features // LANES + 1):
        if features % (pieces * LANES) == 0 and features // pieces <= 4 * LANES:
            chunk = features // pieces
            break
    weight_grad = pl.pallas_call(
        functools.partial(weight_kernel, exp_dev, chunk),
        grid=(exp_dev,),
        out_shape=jax.ShapeDtypeStruct(w_down.shape, jnp.bfloat16),
        in_specs=[
            pl.BlockSpec((1, width, tokens), lambda e: (e, 0, 0)),
            pl.BlockSpec((tokens, features), lambda e: (0, 0)),
            pl.BlockSpec((tokens, LANES), lambda e: (0, 0)),
        ],
        out_specs=pl.BlockSpec((1, width, features), lambda e: (e, 0, 0)),
        compiler_params=pltpu.CompilerParams(vmem_limit_bytes=56 << 20),
        name="weight",
    )(by_token, rows, gates)
    me = lax.axis_index("ctx") * ep_count + lax.axis_index("ep")
    gate_grad = lax.dynamic_slice_in_dim(routes, me * tok_dev, tok_dev, 1).T
    return hid_grad, weight_grad, gate_grad


def route_places(group_ids, experts_all, capacity):
    flat_ids = group_ids.reshape(-1)
    onehot = (flat_ids[:, None] == jnp.arange(experts_all, dtype=jnp.int32)[None, :]).astype(
        jnp.int32
    )
    before = jnp.cumsum(onehot, axis=0) - onehot
    slot_index = jnp.sum(before * onehot, axis=1)
    return (flat_ids * capacity + slot_index).astype(jnp.int32)


def plain_device(out_grad, expert_ids, gate_values, hidden, w_down):
    tok_dev, top_count = expert_ids.shape
    groups, exp_dev, capacity, width_part = hidden.shape
    model_width = out_grad.shape[1]
    ep_count = lax.axis_size("ep")
    ep_rank = lax.axis_index("ep")
    slots_dev = exp_dev * capacity
    experts_all = exp_dev * ep_count
    own_first = ep_rank * slots_dev
    slot_range = jnp.arange(slots_dev, dtype=jnp.int32)
    group_rows, group_ids, group_gates = (
        lax.all_gather(out_grad, "ep", axis=0, tiled=True),
        lax.all_gather(expert_ids, "ep", axis=0, tiled=True),
        lax.all_gather(gate_values.astype(jnp.bfloat16), "ep", axis=0, tiled=True).astype(
            gate_values.dtype
        ),
    )
    places = route_places(group_ids, experts_all, capacity)
    own_places = lax.dynamic_slice_in_dim(
        places, ep_rank * tok_dev * top_count, tok_dev * top_count
    )
    local_slot = places - own_first
    pick_mask = (local_slot[None, :] == slot_range[:, None]).astype(jnp.float32)
    slot_gates = jnp.sum(pick_mask * group_gates.reshape(1, -1), axis=1)
    by_token = pick_mask.reshape(slots_dev, -1, top_count).sum(axis=2).astype(jnp.bfloat16)
    slot_rows = jnp.dot(by_token, group_rows, preferred_element_type=jnp.float32).astype(
        jnp.bfloat16
    )
    stacked_rows = slot_rows.reshape(1, slots_dev, model_width)
    stacked_gates = slot_gates.reshape(1, slots_dev)
    whole_rows, whole_gates = (
        lax.all_gather(stacked_rows, "ctx", axis=0, tiled=True),
        lax.all_gather(stacked_gates.astype(jnp.bfloat16), "ctx", axis=0, tiled=True).astype(
            stacked_gates.dtype
        ),
    )
    row_count = whole_rows.shape[0]
    piece_view = whole_rows.reshape(row_count, exp_dev, capacity, model_width)
    gate_view = whole_gates.reshape(row_count, exp_dev, capacity)
    grad_in = jnp.einsum("necd,efd->necf", piece_view, w_down, preferred_element_type=jnp.float32)
    hid_piece = (gate_view[..., None] * grad_in).astype(jnp.bfloat16)
    gate_piece = jnp.sum(hidden.astype(jnp.float32) * grad_in, axis=3)
    scaled = (gate_view[..., None] * piece_view.astype(jnp.float32)).astype(jnp.bfloat16)
    grad_acc = jnp.einsum("necf,necd->efd", hidden, scaled, preferred_element_type=jnp.float32)
    hid_grad = hid_piece
    partial_value = gate_piece
    grad_acc, hid_grad, partial_value = (grad_acc, hid_grad, partial_value)
    whole_terms = lax.psum(partial_value, "ctx")
    own_terms = lax.dynamic_slice_in_dim(whole_terms, lax.axis_index("ctx"), 1, 0)
    score_table = lax.all_gather(own_terms.reshape(slots_dev), "ep", axis=0, tiled=True)
    lookup = (
        own_places[:, None] == jnp.arange(score_table.shape[0], dtype=jnp.int32)[None, :]
    ).astype(jnp.float32)
    gate_grad = jnp.sum(lookup * score_table[None, :], axis=1).reshape(tok_dev, top_count)
    return (hid_grad, grad_acc.astype(jnp.bfloat16), gate_grad)


def per_device(out_grad, expert_ids, gate_values, hidden, w_down):
    count = lax.axis_size("ctx") * lax.axis_size("ep")
    tokens = count * out_grad.shape[0]
    exp_dev = hidden.shape[1]
    held = 3 * 2 * tokens * out_grad.shape[1] + 2 * w_down.size + 32 * count * tokens
    whole_tiles = out_grad.shape[1] % LANES == 0 and exp_dev <= 8 and hidden.shape[2] <= 8
    body = fused_device if held <= VMEM_BUDGET and whole_tiles else plain_device
    return body(out_grad, expert_ids, gate_values, hidden, w_down)


def solution(mesh):
    placed = (
        P(("ctx", "ep"), None),
        P(("ctx", "ep"), None),
        P(("ctx", "ep"), None),
        P(None, "ep", None, "ctx"),
        P("ep", "ctx", None),
    )
    return jax.shard_map(
        per_device,
        mesh=mesh,
        in_specs=placed,
        out_specs=(P(None, "ep", None, "ctx"), P("ep", "ctx", None), P(("ctx", "ep"), None)),
        check_vma=False,
    )
```

```python
import functools
import jax
import jax.numpy as jnp
from jax import lax
from jax.experimental import pallas as pl
from jax.experimental.pallas import tpu as pltpu
from jax.sharding import PartitionSpec as P

LANES = 128
VMEM_BUDGET = 40 << 20
MESH = pl.DeviceIdType.MESH
HIGHEST = lax.Precision.HIGHEST


def exchange_kernel(
    sizes, grad_ref, ids_ref, gate_ref, hid_ref, w_ref,
    hid_grad_ref, by_token_ref, rows_ref, gates_ref, route_ref,
    pack, rows_in, w_in, part, parts_in,
    w_sem, own_sem, send_sem, recv_sem, pass_sem, passed_sem, send2_sem, recv2_sem,
):
    ctx_count, ep_count, tok_dev, top, groups, exp_dev, capacity, width = sizes
    count = ctx_count * ep_count
    tokens = count * tok_dev
    group_tok = tokens // groups
    features = rows_ref.shape[1]
    ctx, ep = lax.axis_index("ctx"), lax.axis_index("ep")
    me = ctx * ep_count + ep

    def place_of(d):
        return (d // ep_count, lax.rem(d, ep_count))

    def rows_of(d):
        return rows_in.at[d]

    peers = [place_of(lax.rem(me + step, count)) for step in range(1, count)]
    barrier = pltpu.get_barrier_semaphore()
    for peer in peers:
        pl.semaphore_signal(barrier, inc=1, device_id=peer, device_id_type=MESH)
    weights = [
        pltpu.make_async_copy(w_ref.at[e], w_in.at[e], w_sem.at[e]) for e in range(exp_dev)
    ]
    for copy in weights:
        copy.start()
    pack[...] = jnp.concatenate(
        [
            grad_ref[...],
            ids_ref[...].astype(jnp.float32).astype(jnp.bfloat16),
            gate_ref[...].astype(jnp.bfloat16),
            jnp.zeros((tok_dev, LANES - 2 * top), jnp.bfloat16),
        ],
        axis=1,
    )
    pl.semaphore_wait(barrier, count - 1)

    partner = place_of(me + 1 - 2 * lax.rem(me, 2))

    def send(src, d, peer, one, two):
        return pltpu.make_async_remote_copy(
            src_ref=src, dst_ref=rows_of(d), send_sem=one, recv_sem=two,
            device_id=peer, device_id_type=MESH,
        )

    half = count // 2
    sends = [
        send(pack, me, place_of(lax.rem(me + 2 * i, count)), send_sem.at[i - 1], recv_sem.at[i - 1])
        for i in range(1, half)
    ]
    swaps = [send(pack, me, partner, pass_sem.at[0], passed_sem.at[0])]
    for copy in sends + swaps:
        copy.start()
    own = pltpu.make_async_copy(pack, rows_of(me), own_sem)
    own.start()

    pad = 8
    filler = jnp.zeros((pad - exp_dev, width), jnp.float32)
    pieces = []
    for g in range(groups):
        for s in range(capacity):
            pieces += [hid_ref[g, s].astype(jnp.float32)] + ([filler] if pad > exp_dev else [])
    hid = jnp.concatenate(pieces, axis=0).astype(jnp.bfloat16)
    slot_rows = groups * capacity * pad
    tok_a = lax.broadcasted_iota(jnp.int32, (tokens, tokens), 0)
    tok_b = lax.broadcasted_iota(jnp.int32, (tokens, tokens), 1)
    earlier = ((tok_a < tok_b) & (tok_a // group_tok == tok_b // group_tok)).astype(jnp.float32)
    row_slot = lax.broadcasted_iota(jnp.int32, (slot_rows, tokens), 0)
    first = lax.broadcasted_iota(jnp.int32, (1, tokens), 1) // group_tok * (capacity * pad)

    for i in range(1, half):
        sends[i - 1].wait_recv()
        source = lax.rem(me - 2 * i + count, count)
        copy = send(rows_of(source), source, partner, pass_sem.at[i], passed_sem.at[i])
        copy.start()
        swaps.append(copy)
    own.wait()
    for copy in swaps:
        copy.wait_recv()

    gathered = rows_in[...].reshape(tokens, features + LANES)
    rows_ref[...] = gathered[:, :features]
    meta_t = gathered[:, features:].astype(jnp.float32).T
    ids_t = meta_t[:top].astype(jnp.int32)
    gates_t = meta_t[top:2 * top]
    members, gate_rows = [], []
    for e in range(exp_dev):
        named = ids_t == ep * exp_dev + e
        members.append(jnp.sum(jnp.where(named, 1.0, 0.0), axis=0, keepdims=True))
        gate_rows.append(jnp.sum(jnp.where(named, gates_t, 0.0), axis=0, keepdims=True))
    empty = [jnp.zeros((1, tokens), jnp.float32)] * (pad - exp_dev)
    member = jnp.concatenate(members + empty, axis=0)
    gate = jnp.concatenate(gate_rows + empty, axis=0)
    slots = jnp.dot(member, earlier, preferred_element_type=jnp.float32).astype(jnp.int32)
    picks = []
    for e in range(exp_dev):
        place = jnp.where(member[e:e + 1] > 0, first + slots[e:e + 1] * pad + e, -1)
        picks.append(jnp.where(row_slot == place, 1.0, 0.0).astype(jnp.bfloat16))

    gated = []
    for e in range(exp_dev):
        by_token = lax.dot_general(
            hid, picks[e], (((0,), (0,)), ((), ())), preferred_element_type=jnp.float32
        )
        by_token_ref[e] = by_token.astype(jnp.bfloat16)
        weights[e].wait()
        grad = lax.dot_general(
            w_in[e], rows_ref[...], (((1,), (1,)), ((), ())), preferred_element_type=jnp.float32
        )
        part[e:e + 1, :] = jnp.sum(by_token * grad, axis=0, keepdims=True)
        gated.append((grad * gate[e:e + 1]).astype(jnp.bfloat16))

    returns = [
        pltpu.make_async_remote_copy(
            src_ref=part, dst_ref=parts_in.at[me], send_sem=send2_sem.at[i],
            recv_sem=recv2_sem.at[i], device_id=peer, device_id_type=MESH,
        )
        for i, peer in enumerate(peers)
    ]
    for copy in returns:
        copy.start()
    gates_ref[...] = jnp.concatenate(
        [gate, jnp.zeros((LANES - pad, tokens), jnp.float32)], axis=0
    ).T
    slot_grad = jnp.zeros((slot_rows, width), jnp.float32)
    for e in range(exp_dev):
        slot_grad = slot_grad + lax.dot_general(
            picks[e], gated[e], (((1,), (1,)), ((), ())), preferred_element_type=jnp.float32
        )
    for g in range(groups):
        for s in range(capacity):
            at = (g * capacity + s) * pad
            hid_grad_ref[g, s] = slot_grad[at:at + exp_dev].astype(jnp.bfloat16)
    for copy in sends + swaps:
        copy.wait_send()
    for copy in returns:
        copy.wait_recv()
    mine = part[...]
    result = jnp.zeros((top, tokens), jnp.float32)
    for p in range(ep_count):
        total = jnp.zeros(mine.shape, jnp.float32)
        for c in range(ctx_count):
            d = c * ep_count + p
            total = total + jnp.where(d == me, mine, parts_in[d])
        for e in range(exp_dev):
            result = result + jnp.where(ids_t == p * exp_dev + e, total[e:e + 1], 0.0)
    wanted = lax.broadcasted_iota(jnp.int32, (tok_dev, tokens), 0) + me * tok_dev
    chosen = wanted == lax.broadcasted_iota(jnp.int32, (tok_dev, tokens), 1)
    route_ref[...] = lax.dot_general(
        jnp.where(chosen, 1.0, 0.0), result, (((1,), (1,)), ((), ())),
        precision=HIGHEST, preferred_element_type=jnp.float32,
    )
    for copy in returns:
        copy.wait_send()


def weight_kernel(exp_dev, chunk, by_token_ref, rows_ref, gates_ref, out_ref):
    lane = lax.broadcasted_iota(jnp.int32, gates_ref.shape, 1)
    gate = jnp.sum(
        jnp.where(lane == pl.program_id(0), gates_ref[...], 0.0), axis=1, keepdims=True
    )
    left = by_token_ref[0]
    for at in range(0, out_ref.shape[2], chunk):
        scaled = (gate * rows_ref[:, at:at + chunk].astype(jnp.float32)).astype(jnp.bfloat16)
        out_ref[0, :, at:at + chunk] = jnp.dot(
            left, scaled, preferred_element_type=jnp.float32
        ).astype(jnp.bfloat16)


def fused_device(out_grad, expert_ids, gate_values, hidden, w_down):
    tok_dev, top = expert_ids.shape
    groups, exp_dev, capacity, width = hidden.shape
    features = out_grad.shape[1]
    ctx_count, ep_count = lax.axis_size("ctx"), lax.axis_size("ep")
    count = ctx_count * ep_count
    tokens = count * tok_dev
    sizes = (ctx_count, ep_count, tok_dev, top, groups, exp_dev, capacity, width)
    vmem = pl.BlockSpec(memory_space=pltpu.VMEM)
    hid_grad, by_token, rows, gates, routes = pl.pallas_call(
        functools.partial(exchange_kernel, sizes),
        out_shape=(
            jax.ShapeDtypeStruct((groups, capacity, exp_dev, width), jnp.bfloat16),
            jax.ShapeDtypeStruct((exp_dev, width, tokens), jnp.bfloat16),
            jax.ShapeDtypeStruct((tokens, features), jnp.bfloat16),
            jax.ShapeDtypeStruct((tokens, LANES), jnp.float32),
            jax.ShapeDtypeStruct((tok_dev, top), jnp.float32),
        ),
        in_specs=[vmem] * 4 + [pl.BlockSpec(memory_space=pl.ANY)],
        out_specs=(vmem,) * 5,
        scratch_shapes=[
            pltpu.VMEM((tok_dev, features + LANES), jnp.bfloat16),
            pltpu.VMEM((count, tok_dev, features + LANES), jnp.bfloat16),
            pltpu.VMEM(w_down.shape, jnp.bfloat16),
            pltpu.VMEM((exp_dev, tokens), jnp.float32),
            pltpu.VMEM((count, exp_dev, tokens), jnp.float32),
            pltpu.SemaphoreType.DMA((exp_dev,)),
            pltpu.SemaphoreType.DMA,
            pltpu.SemaphoreType.DMA((count // 2 - 1,)),
            pltpu.SemaphoreType.DMA((count // 2 - 1,)),
            pltpu.SemaphoreType.DMA((count // 2,)),
            pltpu.SemaphoreType.DMA((count // 2,)),
            pltpu.SemaphoreType.DMA((count - 1,)),
            pltpu.SemaphoreType.DMA((count - 1,)),
        ],
        compiler_params=pltpu.CompilerParams(
            collective_id=0, has_side_effects=True, vmem_limit_bytes=56 << 20
        ),
        name="exchange",
    )(out_grad, expert_ids, gate_values, jnp.transpose(hidden, (0, 2, 1, 3)), w_down)
    chunk = features
    for pieces in range(1, features // LANES + 1):
        if features % (pieces * LANES) == 0 and features // pieces <= 4 * LANES:
            chunk = features // pieces
            break
    weight_grad = pl.pallas_call(
        functools.partial(weight_kernel, exp_dev, chunk),
        grid=(exp_dev,),
        out_shape=jax.ShapeDtypeStruct(w_down.shape, jnp.bfloat16),
        in_specs=[
            pl.BlockSpec((1, width, tokens), lambda e: (e, 0, 0)),
            pl.BlockSpec((tokens, features), lambda e: (0, 0)),
            pl.BlockSpec((tokens, LANES), lambda e: (0, 0)),
        ],
        out_specs=pl.BlockSpec((1, width, features), lambda e: (e, 0, 0)),
        compiler_params=pltpu.CompilerParams(vmem_limit_bytes=56 << 20),
        name="weight",
    )(by_token, rows, gates)
    return jnp.transpose(hid_grad, (0, 2, 1, 3)), weight_grad, routes


def route_places(group_ids, experts_all, capacity):
    flat_ids = group_ids.reshape(-1)
    onehot = (flat_ids[:, None] == jnp.arange(experts_all, dtype=jnp.int32)[None, :]).astype(
        jnp.int32
    )
    before = jnp.cumsum(onehot, axis=0) - onehot
    slot_index = jnp.sum(before * onehot, axis=1)
    return (flat_ids * capacity + slot_index).astype(jnp.int32)


def plain_device(out_grad, expert_ids, gate_values, hidden, w_down):
    tok_dev, top_count = expert_ids.shape
    groups, exp_dev, capacity, width_part = hidden.shape
    model_width = out_grad.shape[1]
    ep_count = lax.axis_size("ep")
    ep_rank = lax.axis_index("ep")
    slots_dev = exp_dev * capacity
    experts_all = exp_dev * ep_count
    own_first = ep_rank * slots_dev
    slot_range = jnp.arange(slots_dev, dtype=jnp.int32)
    group_rows, group_ids, group_gates = (
        lax.all_gather(out_grad, "ep", axis=0, tiled=True),
        lax.all_gather(expert_ids, "ep", axis=0, tiled=True),
        lax.all_gather(gate_values.astype(jnp.bfloat16), "ep", axis=0, tiled=True).astype(
            gate_values.dtype
        ),
    )
    places = route_places(group_ids, experts_all, capacity)
    own_places = lax.dynamic_slice_in_dim(
        places, ep_rank * tok_dev * top_count, tok_dev * top_count
    )
    local_slot = places - own_first
    pick_mask = (local_slot[None, :] == slot_range[:, None]).astype(jnp.float32)
    slot_gates = jnp.sum(pick_mask * group_gates.reshape(1, -1), axis=1)
    by_token = pick_mask.reshape(slots_dev, -1, top_count).sum(axis=2).astype(jnp.bfloat16)
    slot_rows = jnp.dot(by_token, group_rows, preferred_element_type=jnp.float32).astype(
        jnp.bfloat16
    )
    stacked_rows = slot_rows.reshape(1, slots_dev, model_width)
    stacked_gates = slot_gates.reshape(1, slots_dev)
    whole_rows, whole_gates = (
        lax.all_gather(stacked_rows, "ctx", axis=0, tiled=True),
        lax.all_gather(stacked_gates.astype(jnp.bfloat16), "ctx", axis=0, tiled=True).astype(
            stacked_gates.dtype
        ),
    )
    row_count = whole_rows.shape[0]
    piece_view = whole_rows.reshape(row_count, exp_dev, capacity, model_width)
    gate_view = whole_gates.reshape(row_count, exp_dev, capacity)
    grad_in = jnp.einsum("necd,efd->necf", piece_view, w_down, preferred_element_type=jnp.float32)
    hid_piece = (gate_view[..., None] * grad_in).astype(jnp.bfloat16)
    gate_piece = jnp.sum(hidden.astype(jnp.float32) * grad_in, axis=3)
    scaled = (gate_view[..., None] * piece_view.astype(jnp.float32)).astype(jnp.bfloat16)
    grad_acc = jnp.einsum("necf,necd->efd", hidden, scaled, preferred_element_type=jnp.float32)
    hid_grad = hid_piece
    partial_value = gate_piece
    grad_acc, hid_grad, partial_value = (grad_acc, hid_grad, partial_value)
    whole_terms = lax.psum(partial_value, "ctx")
    own_terms = lax.dynamic_slice_in_dim(whole_terms, lax.axis_index("ctx"), 1, 0)
    score_table = lax.all_gather(own_terms.reshape(slots_dev), "ep", axis=0, tiled=True)
    lookup = (
        own_places[:, None] == jnp.arange(score_table.shape[0], dtype=jnp.int32)[None, :]
    ).astype(jnp.float32)
    gate_grad = jnp.sum(lookup * score_table[None, :], axis=1).reshape(tok_dev, top_count)
    return (hid_grad, grad_acc.astype(jnp.bfloat16), gate_grad)


def per_device(out_grad, expert_ids, gate_values, hidden, w_down):
    count = lax.axis_size("ctx") * lax.axis_size("ep")
    tokens = count * out_grad.shape[0]
    exp_dev = hidden.shape[1]
    held = 3 * 2 * tokens * out_grad.shape[1] + 2 * w_down.size + 32 * count * tokens
    whole_tiles = count % 2 == 0 and out_grad.shape[1] % LANES == 0 and exp_dev <= 8 and hidden.shape[2] <= 8
    body = fused_device if held <= VMEM_BUDGET and whole_tiles else plain_device
    return body(out_grad, expert_ids, gate_values, hidden, w_down)


def solution(mesh):
    placed = (
        P(("ctx", "ep"), None),
        P(("ctx", "ep"), None),
        P(("ctx", "ep"), None),
        P(None, "ep", None, "ctx"),
        P("ep", "ctx", None),
    )
    return jax.shard_map(
        per_device,
        mesh=mesh,
        in_specs=placed,
        out_specs=(P(None, "ep", None, "ctx"), P("ep", "ctx", None), P(("ctx", "ep"), None)),
        check_vma=False,
    )
```

```python
import functools
import jax
import jax.numpy as jnp
from jax import lax
from jax.experimental import pallas as pl
from jax.experimental.pallas import tpu as pltpu
from jax.sharding import PartitionSpec as P

LANES = 128
VMEM_BUDGET = 40 << 20
MESH = pl.DeviceIdType.MESH
HIGHEST = lax.Precision.HIGHEST


def exchange_kernel(
    sizes, grad_ref, ids_ref, gate_ref, hid_ref, w_ref,
    hid_grad_ref, by_token_ref, rows_ref, gates_ref, route_ref,
    pack, rows_in, w_in, part, parts_in,
    w_sem, own_sem, send_sem, recv_sem, pass_sem, passed_sem, send2_sem, recv2_sem,
):
    ctx_count, ep_count, tok_dev, top, groups, exp_dev, capacity, width = sizes
    count = ctx_count * ep_count
    tokens = count * tok_dev
    group_tok = tokens // groups
    features = rows_ref.shape[1]
    ctx, ep = lax.axis_index("ctx"), lax.axis_index("ep")
    me = ctx * ep_count + ep

    def place_of(d):
        return (d // ep_count, lax.rem(d, ep_count))

    def rows_of(d):
        return rows_in.at[pl.ds(pl.multiple_of(d * tok_dev, tok_dev), tok_dev), :]

    peers = [place_of(lax.rem(me + step, count)) for step in range(1, count)]
    barrier = pltpu.get_barrier_semaphore()
    for peer in peers:
        pl.semaphore_signal(barrier, inc=1, device_id=peer, device_id_type=MESH)
    weights = [
        pltpu.make_async_copy(w_ref.at[e], w_in.at[e], w_sem.at[e]) for e in range(exp_dev)
    ]
    for copy in weights:
        copy.start()
    pack[...] = jnp.concatenate(
        [
            grad_ref[...],
            ids_ref[...].astype(jnp.float32).astype(jnp.bfloat16),
            gate_ref[...].astype(jnp.bfloat16),
            jnp.zeros((tok_dev, LANES - 2 * top), jnp.bfloat16),
        ],
        axis=1,
    )
    pl.semaphore_wait(barrier, count - 1)

    partner = place_of(me + 1 - 2 * lax.rem(me, 2))

    def send(src, d, peer, one, two):
        return pltpu.make_async_remote_copy(
            src_ref=src, dst_ref=rows_of(d), send_sem=one, recv_sem=two,
            device_id=peer, device_id_type=MESH,
        )

    half = count // 2
    sends = [
        send(pack, me, place_of(lax.rem(me + 2 * i, count)), send_sem.at[i - 1], recv_sem.at[i - 1])
        for i in range(1, half)
    ]
    swaps = [send(pack, me, partner, pass_sem.at[0], passed_sem.at[0])]
    for copy in sends + swaps:
        copy.start()
    own = pltpu.make_async_copy(pack, rows_of(me), own_sem)
    own.start()

    pad = 8
    filler = jnp.zeros((pad - exp_dev, width), jnp.float32)
    pieces = []
    for g in range(groups):
        for s in range(capacity):
            pieces += [hid_ref[g, s].astype(jnp.float32)] + ([filler] if pad > exp_dev else [])
    hid = jnp.concatenate(pieces, axis=0).astype(jnp.bfloat16)
    slot_rows = groups * capacity * pad
    tok_a = lax.broadcasted_iota(jnp.int32, (tokens, tokens), 0)
    tok_b = lax.broadcasted_iota(jnp.int32, (tokens, tokens), 1)
    earlier = ((tok_a < tok_b) & (tok_a // group_tok == tok_b // group_tok)).astype(jnp.float32)
    row_slot = lax.broadcasted_iota(jnp.int32, (slot_rows, tokens), 0)
    first = lax.broadcasted_iota(jnp.int32, (1, tokens), 1) // group_tok * (capacity * pad)

    for i in range(1, half):
        sends[i - 1].wait_recv()
        source = lax.rem(me - 2 * i + count, count)
        copy = send(rows_of(source), source, partner, pass_sem.at[i], passed_sem.at[i])
        copy.start()
        swaps.append(copy)
    own.wait()
    for copy in swaps:
        copy.wait_recv()

    gathered = rows_in[...]
    rows_ref[...] = gathered[:, :features]
    meta_t = gathered[:, features:].astype(jnp.float32).T
    ids_t = meta_t[:top].astype(jnp.int32)
    gates_t = meta_t[top:2 * top]
    members, gate_rows = [], []
    for e in range(exp_dev):
        named = ids_t == ep * exp_dev + e
        members.append(jnp.sum(jnp.where(named, 1.0, 0.0), axis=0, keepdims=True))
        gate_rows.append(jnp.sum(jnp.where(named, gates_t, 0.0), axis=0, keepdims=True))
    empty = [jnp.zeros((1, tokens), jnp.float32)] * (pad - exp_dev)
    member = jnp.concatenate(members + empty, axis=0)
    gate = jnp.concatenate(gate_rows + empty, axis=0)
    slots = jnp.dot(member, earlier, preferred_element_type=jnp.float32).astype(jnp.int32)
    picks = []
    for e in range(exp_dev):
        place = jnp.where(member[e:e + 1] > 0, first + slots[e:e + 1] * pad + e, -1)
        picks.append(jnp.where(row_slot == place, 1.0, 0.0).astype(jnp.bfloat16))

    gated = []
    for e in range(exp_dev):
        by_token = lax.dot_general(
            hid, picks[e], (((0,), (0,)), ((), ())), preferred_element_type=jnp.float32
        )
        by_token_ref[e] = by_token.astype(jnp.bfloat16)
        weights[e].wait()
        grad = lax.dot_general(
            w_in[e], rows_ref[...], (((1,), (1,)), ((), ())), preferred_element_type=jnp.float32
        )
        part[e:e + 1, :] = jnp.sum(by_token * grad, axis=0, keepdims=True)
        gated.append((grad * gate[e:e + 1]).astype(jnp.bfloat16))

    returns = [
        pltpu.make_async_remote_copy(
            src_ref=part, dst_ref=parts_in.at[me], send_sem=send2_sem.at[i],
            recv_sem=recv2_sem.at[i], device_id=peer, device_id_type=MESH,
        )
        for i, peer in enumerate(peers)
    ]
    for copy in returns:
        copy.start()
    gates_ref[...] = jnp.concatenate(
        [gate, jnp.zeros((LANES - pad, tokens), jnp.float32)], axis=0
    ).T
    slot_grad = jnp.zeros((slot_rows, width), jnp.float32)
    for e in range(exp_dev):
        slot_grad = slot_grad + lax.dot_general(
            picks[e], gated[e], (((1,), (1,)), ((), ())), preferred_element_type=jnp.float32
        )
    for g in range(groups):
        for s in range(capacity):
            at = (g * capacity + s) * pad
            hid_grad_ref[g, s] = slot_grad[at:at + exp_dev].astype(jnp.bfloat16)
    for copy in sends + swaps:
        copy.wait_send()
    for copy in returns:
        copy.wait_recv()
    mine = part[...]
    result = jnp.zeros((top, tokens), jnp.float32)
    for p in range(ep_count):
        total = jnp.zeros(mine.shape, jnp.float32)
        for c in range(ctx_count):
            d = c * ep_count + p
            total = total + jnp.where(d == me, mine, parts_in[d])
        for e in range(exp_dev):
            result = result + jnp.where(ids_t == p * exp_dev + e, total[e:e + 1], 0.0)
    wanted = lax.broadcasted_iota(jnp.int32, (tok_dev, tokens), 0) + me * tok_dev
    chosen = wanted == lax.broadcasted_iota(jnp.int32, (tok_dev, tokens), 1)
    route_ref[...] = lax.dot_general(
        jnp.where(chosen, 1.0, 0.0), result, (((1,), (1,)), ((), ())),
        precision=HIGHEST, preferred_element_type=jnp.float32,
    )
    for copy in returns:
        copy.wait_send()


def weight_kernel(exp_dev, chunk, by_token_ref, rows_ref, gates_ref, out_ref):
    lane = lax.broadcasted_iota(jnp.int32, gates_ref.shape, 1)
    gate = jnp.sum(
        jnp.where(lane == pl.program_id(0), gates_ref[...], 0.0), axis=1, keepdims=True
    )
    left = by_token_ref[0]
    for at in range(0, out_ref.shape[2], chunk):
        scaled = (gate * rows_ref[:, at:at + chunk].astype(jnp.float32)).astype(jnp.bfloat16)
        out_ref[0, :, at:at + chunk] = jnp.dot(
            left, scaled, preferred_element_type=jnp.float32
        ).astype(jnp.bfloat16)


def fused_device(out_grad, expert_ids, gate_values, hidden, w_down):
    tok_dev, top = expert_ids.shape
    groups, exp_dev, capacity, width = hidden.shape
    features = out_grad.shape[1]
    ctx_count, ep_count = lax.axis_size("ctx"), lax.axis_size("ep")
    count = ctx_count * ep_count
    tokens = count * tok_dev
    sizes = (ctx_count, ep_count, tok_dev, top, groups, exp_dev, capacity, width)
    vmem = pl.BlockSpec(memory_space=pltpu.VMEM)
    hid_grad, by_token, rows, gates, routes = pl.pallas_call(
        functools.partial(exchange_kernel, sizes),
        out_shape=(
            jax.ShapeDtypeStruct((groups, capacity, exp_dev, width), jnp.bfloat16),
            jax.ShapeDtypeStruct((exp_dev, width, tokens), jnp.bfloat16),
            jax.ShapeDtypeStruct((tokens, features), jnp.bfloat16),
            jax.ShapeDtypeStruct((tokens, LANES), jnp.float32),
            jax.ShapeDtypeStruct((tok_dev, top), jnp.float32),
        ),
        in_specs=[vmem] * 4 + [pl.BlockSpec(memory_space=pl.ANY)],
        out_specs=(vmem,) * 5,
        scratch_shapes=[
            pltpu.VMEM((tok_dev, features + LANES), jnp.bfloat16),
            pltpu.VMEM((tokens, features + LANES), jnp.bfloat16),
            pltpu.VMEM(w_down.shape, jnp.bfloat16),
            pltpu.VMEM((exp_dev, tokens), jnp.float32),
            pltpu.VMEM((count, exp_dev, tokens), jnp.float32),
            pltpu.SemaphoreType.DMA((exp_dev,)),
            pltpu.SemaphoreType.DMA,
            pltpu.SemaphoreType.DMA((count // 2 - 1,)),
            pltpu.SemaphoreType.DMA((count // 2 - 1,)),
            pltpu.SemaphoreType.DMA((count // 2,)),
            pltpu.SemaphoreType.DMA((count // 2,)),
            pltpu.SemaphoreType.DMA((count - 1,)),
            pltpu.SemaphoreType.DMA((count - 1,)),
        ],
        compiler_params=pltpu.CompilerParams(
            collective_id=0, has_side_effects=True, vmem_limit_bytes=56 << 20
        ),
        name="exchange",
    )(out_grad, expert_ids, gate_values, jnp.transpose(hidden, (0, 2, 1, 3)), w_down)
    chunk = features
    for pieces in range(1, features // LANES + 1):
        if features % (pieces * LANES) == 0 and features // pieces <= 4 * LANES:
            chunk = features // pieces
            break
    weight_grad = pl.pallas_call(
        functools.partial(weight_kernel, exp_dev, chunk),
        grid=(exp_dev,),
        out_shape=jax.ShapeDtypeStruct(w_down.shape, jnp.bfloat16),
        in_specs=[
            pl.BlockSpec((1, width, tokens), lambda e: (e, 0, 0)),
            pl.BlockSpec((tokens, features), lambda e: (0, 0)),
            pl.BlockSpec((tokens, LANES), lambda e: (0, 0)),
        ],
        out_specs=pl.BlockSpec((1, width, features), lambda e: (e, 0, 0)),
        compiler_params=pltpu.CompilerParams(vmem_limit_bytes=56 << 20),
        name="weight",
    )(by_token, rows, gates)
    return jnp.transpose(hid_grad, (0, 2, 1, 3)), weight_grad, routes


def route_places(group_ids, experts_all, capacity):
    flat_ids = group_ids.reshape(-1)
    onehot = (flat_ids[:, None] == jnp.arange(experts_all, dtype=jnp.int32)[None, :]).astype(
        jnp.int32
    )
    before = jnp.cumsum(onehot, axis=0) - onehot
    slot_index = jnp.sum(before * onehot, axis=1)
    return (flat_ids * capacity + slot_index).astype(jnp.int32)


def plain_device(out_grad, expert_ids, gate_values, hidden, w_down):
    tok_dev, top_count = expert_ids.shape
    groups, exp_dev, capacity, width_part = hidden.shape
    model_width = out_grad.shape[1]
    ep_count = lax.axis_size("ep")
    ep_rank = lax.axis_index("ep")
    slots_dev = exp_dev * capacity
    experts_all = exp_dev * ep_count
    own_first = ep_rank * slots_dev
    slot_range = jnp.arange(slots_dev, dtype=jnp.int32)
    group_rows, group_ids, group_gates = (
        lax.all_gather(out_grad, "ep", axis=0, tiled=True),
        lax.all_gather(expert_ids, "ep", axis=0, tiled=True),
        lax.all_gather(gate_values.astype(jnp.bfloat16), "ep", axis=0, tiled=True).astype(
            gate_values.dtype
        ),
    )
    places = route_places(group_ids, experts_all, capacity)
    own_places = lax.dynamic_slice_in_dim(
        places, ep_rank * tok_dev * top_count, tok_dev * top_count
    )
    local_slot = places - own_first
    pick_mask = (local_slot[None, :] == slot_range[:, None]).astype(jnp.float32)
    slot_gates = jnp.sum(pick_mask * group_gates.reshape(1, -1), axis=1)
    by_token = pick_mask.reshape(slots_dev, -1, top_count).sum(axis=2).astype(jnp.bfloat16)
    slot_rows = jnp.dot(by_token, group_rows, preferred_element_type=jnp.float32).astype(
        jnp.bfloat16
    )
    stacked_rows = slot_rows.reshape(1, slots_dev, model_width)
    stacked_gates = slot_gates.reshape(1, slots_dev)
    whole_rows, whole_gates = (
        lax.all_gather(stacked_rows, "ctx", axis=0, tiled=True),
        lax.all_gather(stacked_gates.astype(jnp.bfloat16), "ctx", axis=0, tiled=True).astype(
            stacked_gates.dtype
        ),
    )
    row_count = whole_rows.shape[0]
    piece_view = whole_rows.reshape(row_count, exp_dev, capacity, model_width)
    gate_view = whole_gates.reshape(row_count, exp_dev, capacity)
    grad_in = jnp.einsum("necd,efd->necf", piece_view, w_down, preferred_element_type=jnp.float32)
    hid_piece = (gate_view[..., None] * grad_in).astype(jnp.bfloat16)
    gate_piece = jnp.sum(hidden.astype(jnp.float32) * grad_in, axis=3)
    scaled = (gate_view[..., None] * piece_view.astype(jnp.float32)).astype(jnp.bfloat16)
    grad_acc = jnp.einsum("necf,necd->efd", hidden, scaled, preferred_element_type=jnp.float32)
    hid_grad = hid_piece
    partial_value = gate_piece
    grad_acc, hid_grad, partial_value = (grad_acc, hid_grad, partial_value)
    whole_terms = lax.psum(partial_value, "ctx")
    own_terms = lax.dynamic_slice_in_dim(whole_terms, lax.axis_index("ctx"), 1, 0)
    score_table = lax.all_gather(own_terms.reshape(slots_dev), "ep", axis=0, tiled=True)
    lookup = (
        own_places[:, None] == jnp.arange(score_table.shape[0], dtype=jnp.int32)[None, :]
    ).astype(jnp.float32)
    gate_grad = jnp.sum(lookup * score_table[None, :], axis=1).reshape(tok_dev, top_count)
    return (hid_grad, grad_acc.astype(jnp.bfloat16), gate_grad)


def per_device(out_grad, expert_ids, gate_values, hidden, w_down):
    count = lax.axis_size("ctx") * lax.axis_size("ep")
    tokens = count * out_grad.shape[0]
    exp_dev = hidden.shape[1]
    held = 3 * 2 * tokens * out_grad.shape[1] + 2 * w_down.size + 32 * count * tokens
    whole_tiles = count % 2 == 0 and out_grad.shape[1] % LANES == 0 and exp_dev <= 8 and hidden.shape[2] <= 8
    body = fused_device if held <= VMEM_BUDGET and whole_tiles else plain_device
    return body(out_grad, expert_ids, gate_values, hidden, w_down)


def solution(mesh):
    placed = (
        P(("ctx", "ep"), None),
        P(("ctx", "ep"), None),
        P(("ctx", "ep"), None),
        P(None, "ep", None, "ctx"),
        P("ep", "ctx", None),
    )
    return jax.shard_map(
        per_device,
        mesh=mesh,
        in_specs=placed,
        out_specs=(P(None, "ep", None, "ctx"), P("ep", "ctx", None), P(("ctx", "ep"), None)),
        check_vma=False,
    )
```
